32 devices in a mesh: grp: 2 (over x), blk: 16 (over z, y, core).
Axes of the slice: x: 2, y: 2, z: 4, core: 2. Of those that a mesh axis runs over, the one named last changes fastest.
Arguments:
- theta: bfloat16 [32, 1024, 128], P(('grp', 'blk')), parts along dimension 0, may hold values from -6 to 6
- trial: bfloat16 [2048, 128], P('grp'), parts along dimension 0, may hold values from -0.5 to 0.5
- chol: bfloat16 [64, 128, 16384], P(('grp', 'blk')), parts along dimension 0, may hold values from -0.009765625 to 0.009765625
- fields: float32 [32, 128], P(('grp', 'blk')), parts along dimension 0, may hold values from -6 to 6
- tile_info: int32 [6, 32], P('grp'), parts along dimension 0, may hold values from 0 to 7, as said below
- tile_count: int32 [32], P('grp'), parts along dimension 0, may hold values from 0 to 2
- block_size: int32 [16], P('grp'), parts along dimension 0, may hold values from 96 to 128
Outputs:
- propagated: bfloat16 [32, 1024, 128], P(('grp', 'blk')), parts along dimension 0
- force_bias: float32 [32, 128], P(('grp', 'blk')), parts along dimension 0
The draws below stay inside these ranges and needn't reach their ends.
There are 2 independent parts, one for each index of `grp`. The reference program is written for one: setup_inputs(seed, part) draws one part's arguments, and reference() takes and returns one part's arrays. A program takes and returns all parts, laid end to end along the dimension named above; each array names one. Nothing has to cross between parts.
Inputs may be any that keep to these rules, and one draw needn't show every extreme that they name: `tile_info`: every pair of blocks (P, Q) with |P - Q| <= 1 and every vector range below 1 stand in exactly one live slot; live slots of an owner come first; unused slots hold zeros.
All inputs are finite; a program needn't handle non-finite values.
Results may differ from the reference program's by a relative error of at most 0.0045.
Values may be sent and summed in bfloat16 or wider, within the bound.
A program may use at most 128 MiB of HBM per device.

```python
import jax
import jax.numpy as jnp
from jax import lax

BS = 128
NBLOCK = 8
NOCC = 128
GS = 128
TMAX = 2
NORB = 1024
NPAIR = 22
NSLAB = 1
NCHOL = 128
WALKERS = 16
N_BLK = 16


def tile_layout(key):
    layout_key = jax.random.fold_in(key, 11)
    slot_total = N_BLK * TMAX
    tile_total = NPAIR * NSLAB
    shuffled = jax.random.permutation(layout_key, slot_total).astype(jnp.int32).reshape(N_BLK, TMAX)
    live_slots = shuffled < tile_total
    ordering = jnp.argsort(jnp.where(live_slots, 0, 1).astype(jnp.int32), axis=1, stable=True)
    packed = jnp.take_along_axis(shuffled, ordering, axis=1)
    alive = jnp.take_along_axis(live_slots, ordering, axis=1)
    live_count = jnp.sum(alive.astype(jnp.int32), axis=1).astype(jnp.int32)
    alive_flat = alive.reshape(slot_total)
    tile_ids = jnp.where(alive_flat, packed.reshape(slot_total), 0)
    pair_ids = tile_ids % NPAIR
    slab_ids = tile_ids // NPAIR
    upper_off = pair_ids - NBLOCK
    lower_off = pair_ids - (2 * NBLOCK - 1)
    row_ids = jnp.where(pair_ids < NBLOCK, pair_ids, jnp.where(lower_off < 0, upper_off, lower_off + 1))
    col_ids = jnp.where(pair_ids < NBLOCK, pair_ids, jnp.where(lower_off < 0, upper_off + 1, lower_off))
    live_int = alive_flat.astype(jnp.int32)
    tile_table = jnp.stack([row_ids * live_int, col_ids * live_int, slab_ids * live_int]).astype(jnp.int32)
    return (tile_table, live_count)


def draw_tile_info(key, part):
    return tile_layout(key)[0]


def draw_tile_count(key, part):
    return tile_layout(key)[1]


def draw_block_size(key, part):
    size_key = jax.random.fold_in(key, 23)
    place_key = jax.random.fold_in(key, 29)
    sizes = jax.random.randint(size_key, (NBLOCK,), BS - BS // 4, BS).astype(jnp.int32)
    chosen = jax.random.randint(place_key, (), 0, NBLOCK).astype(jnp.int32)
    return jnp.where(jnp.arange(NBLOCK, dtype=jnp.int32) == chosen, BS, sizes).astype(jnp.int32)


def block_levels(key, dims, split, smallest, largest):
    loudness, own = 1.0, jax.random.fold_in(key, 6)
    for dim, blocks in split:
        draws = jnp.exp(jax.random.uniform(jax.random.fold_in(own, dim), (blocks,), jnp.float32, smallest / len(split), largest / len(split)))
        loudness = loudness * jnp.repeat(draws, dims[dim] // blocks).reshape([-1 if axis == dim else 1 for axis in range(len(dims))])
    return loudness


def centred(own_key, extent, width, limit, pieces=(), kind=jnp.bfloat16):
    level = block_levels(own_key, extent, pieces, -0.22, 0.18) if pieces else 1.0
    drawn = jax.random.normal(own_key, extent, jnp.float32) * width * level
    return jnp.minimum(jnp.maximum(drawn, -limit), limit).astype(kind)


def setup_inputs(seed: int = 0, part: int = 0) -> dict:
    key_list = jax.random.split(jax.random.key(seed), 8)
    own_keys = jax.random.split(jax.random.fold_in(key_list[7], part), 8)
    theta = centred(own_keys[0], (WALKERS, NORB, NOCC), 1.0, 6.0, ((0, 16),))
    trial = centred(own_keys[1], (NORB, NOCC), NOCC ** -0.5, 0.5)
    chol = centred(own_keys[2], (N_BLK * TMAX, GS, BS * BS), (NPAIR * BS * BS) ** -0.5, 0.009765625, ((0, 16),))
    fields = centred(own_keys[3], (WALKERS, NCHOL), 1.0, 6.0, ((0, 16),), jnp.float32)
    tile_info = draw_tile_info(jax.random.fold_in(jax.random.fold_in(key_list[7], part), 71), part)
    tile_count = draw_tile_count(jax.random.fold_in(jax.random.fold_in(key_list[7], part), 71), part)
    block_size = draw_block_size(jax.random.fold_in(jax.random.fold_in(key_list[7], part), 71), part)
    return {"theta": theta, "trial": trial, "chol": chol, "fields": fields, "tile_info": tile_info, "tile_count": tile_count, "block_size": block_size}


step_root = 0.25


def reference(theta, trial, chol, fields, tile_info, tile_count, block_size):
    walkers = theta.shape[0]
    slot_total = chol.shape[0]
    zero_index = jnp.zeros((), jnp.int32)
    rows_valid = (jnp.arange(BS, dtype=jnp.int32)[None, :] < block_size[:, None]).astype(jnp.float32)
    slot_ids = jnp.arange(slot_total, dtype=jnp.int32)
    slot_live = ((slot_ids % TMAX) < tile_count[slot_ids // TMAX]).astype(jnp.float32)
    theta_wide = theta.astype(jnp.float32)
    trial_wide = trial.astype(jnp.float32)

    def tile_parts(slot_index):
        row_block = tile_info[0, slot_index]
        col_block = tile_info[1, slot_index]
        slab_index = tile_info[2, slot_index]
        trial_rows = lax.dynamic_slice(trial_wide, (row_block * BS, zero_index), (BS, NOCC))
        theta_rows = lax.dynamic_slice(theta_wide, (zero_index, col_block * BS, zero_index), (walkers, BS, NOCC))
        valid_mask = rows_valid[row_block][:, None] * rows_valid[col_block][None, :] * slot_live[slot_index]
        cholesky_tile = chol[slot_index].astype(jnp.float32)
        return row_block, slab_index, trial_rows, theta_rows, valid_mask, cholesky_tile

    def bias_step(slot_index, bias_total):
        parts = tile_parts(slot_index)
        slab_index, trial_rows, theta_rows, valid_mask, cholesky_tile = parts[1], parts[2], parts[3], parts[4], parts[5]
        green_block = (jnp.einsum("pk,wqk->wpq", trial_rows, theta_rows) * valid_mask).astype(jnp.bfloat16)
        bias_term = jnp.einsum("wf,gf->wg", green_block.reshape(walkers, BS * BS).astype(jnp.float32), cholesky_tile)
        current = lax.dynamic_slice(bias_total, (zero_index, slab_index * GS), (walkers, GS))
        return lax.dynamic_update_slice(bias_total, current + bias_term, (zero_index, slab_index * GS))

    force_bias = lax.fori_loop(jnp.int32(0), jnp.int32(slot_total), bias_step,
                               jnp.zeros((walkers, fields.shape[1]), jnp.float32))
    shifted = (fields - force_bias).astype(jnp.bfloat16)
    shifted_wide = shifted.astype(jnp.float32)

    def update_step(slot_index, update):
        row_block, slab_index, trial_rows, theta_rows, valid_mask, cholesky_tile = tile_parts(slot_index)
        field_slab = lax.dynamic_slice(shifted_wide, (zero_index, slab_index * GS), (walkers, GS))
        operator_block = ((jnp.einsum("wg,gf->wf", field_slab, cholesky_tile) * step_root).reshape(walkers, BS, BS) * valid_mask).astype(jnp.bfloat16)
        contribution = jnp.einsum("wpq,wqk->wpk", operator_block.astype(jnp.float32), theta_rows)
        current = lax.dynamic_slice(update, (zero_index, row_block * BS, zero_index), (walkers, BS, NOCC))
        return lax.dynamic_update_slice(update, current + contribution, (zero_index, row_block * BS, zero_index))

    update = lax.fori_loop(jnp.int32(0), jnp.int32(slot_total), update_step, jnp.zeros(theta.shape, jnp.float32))
    propagated = (theta_wide + update).astype(jnp.bfloat16)
    return (propagated, force_bias)
```

```python
import functools

import jax
import jax.numpy as jnp
from jax import lax
from jax.experimental import pallas as pl
from jax.experimental.pallas import tpu as pltpu
from jax.sharding import PartitionSpec as P

BS = 128
NBLOCK = 8
NOCC = 128
GS = 128
TMAX = 2


step_root = 0.25

CHUNK = 8
VMEM_LIMIT = 60000 * 1024
MESH = pl.DeviceIdType.MESH


def fused_kernel(
    n,
    nslab,
    info_ref,
    count_ref,
    size_ref,
    slot_of_ref,
    theta_ref,
    trial_ref,
    fields_ref,
    chol_ref,
    prop_ref,
    bias_ref,
    chol_v,
    staged,
    received,
    wide,
    part,
    parts_all,
    total_ref,
    fields_all,
    ops_out,
    ops_in,
    chol_sem,
    theta_send,
    theta_recv,
    field_send,
    field_recv,
    bias_send,
    bias_recv,
    op_send,
    op_recv,
):
    me = lax.axis_index("blk")
    grp = lax.axis_index("grp")

    def peer(step):
        return lax.rem(me + step, n)

    def each_peer(body):
        def run(step, carry):
            body(peer(step))
            return carry

        lax.fori_loop(1, n, run, 0)

    def theta_copy(slot, src, dst):
        return pltpu.make_async_remote_copy(
            src_ref=staged.at[slot, dst],
            dst_ref=received.at[slot, src],
            send_sem=theta_send.at[slot, dst],
            recv_sem=theta_recv.at[slot, src],
            device_id=(grp, dst),
            device_id_type=MESH,
        )

    def field_copy(src, dst):
        return pltpu.make_async_remote_copy(
            src_ref=fields_ref,
            dst_ref=fields_all.at[src],
            send_sem=field_send.at[dst],
            recv_sem=field_recv.at[src],
            device_id=(grp, dst),
            device_id_type=MESH,
        )

    def bias_copy(src, dst):
        return pltpu.make_async_remote_copy(
            src_ref=part,
            dst_ref=parts_all.at[src],
            send_sem=bias_send.at[dst],
            recv_sem=bias_recv.at[src],
            device_id=(grp, dst),
            device_id_type=MESH,
        )

    def op_copy(slot, src, dst):
        return pltpu.make_async_remote_copy(
            src_ref=ops_out.at[slot, dst],
            dst_ref=ops_in.at[slot * n + src],
            send_sem=op_send.at[slot, dst],
            recv_sem=op_recv.at[slot, src],
            device_id=(grp, dst),
            device_id_type=MESH,
        )

    barrier = pltpu.get_barrier_semaphore()
    each_peer(
        lambda dst: pl.semaphore_signal(
            barrier, inc=1, device_id=(grp, dst), device_id_type=MESH
        )
    )
    chol_loads = [
        pltpu.make_async_copy(chol_ref.at[slot], chol_v.at[slot], chol_sem.at[slot])
        for slot in range(TMAX)
    ]
    for load in chol_loads:
        load.start()

    def stage(owner, carry):
        for slot in range(TMAX):
            col = info_ref[1, owner * TMAX + slot]
            staged[slot, owner] = theta_ref[col]
        return carry

    lax.fori_loop(0, n, stage, 0)
    for slot in range(TMAX):
        received[slot, me] = staged[slot, me]
    fields_all[me] = fields_ref[...]
    part[...] = jnp.zeros_like(part)

    pl.semaphore_wait(barrier, n - 1)
    for slot in range(TMAX):
        each_peer(lambda dst: theta_copy(slot, me, dst).start())
        if slot == 0:
            each_peer(lambda dst: field_copy(me, dst).start())

    row_ids = lax.broadcasted_iota(jnp.int32, (BS, BS), 0)
    col_ids = lax.broadcasted_iota(jnp.int32, (BS, BS), 1)

    def slab_ids(slab):
        return jnp.broadcast_to(slab, (n, GS))

    def slot_facts(slot):
        own = me * TMAX + slot
        row = info_ref[0, own]
        col = info_ref[1, own]
        live = jnp.broadcast_to(count_ref[me], (BS, BS)) > slot
        valid = (row_ids < size_ref[row]) & (col_ids < size_ref[col]) & live
        return row, info_ref[2, own], valid.astype(jnp.float32)

    for slot in range(TMAX):
        row, slab, valid = slot_facts(slot)
        trial_rows = trial_ref[row]
        each_peer(lambda src: theta_copy(slot, src, me).wait_recv())

        def green_step(walker, carry):
            green = lax.dot_general(
                trial_rows,
                received[slot, walker],
                (((1,), (1,)), ((), ())),
                preferred_element_type=jnp.float32,
            )
            green = (green * valid).astype(jnp.bfloat16).astype(jnp.float32)
            wide[pl.ds(pl.multiple_of(walker * BS, BS), BS), :] = green
            return carry

        lax.fori_loop(0, n, green_step, 0, unroll=4)
        chol_loads[slot].wait()

        def bias_step(chunk, acc):
            left = jnp.concatenate(
                [wide[pl.ds(chunk * CHUNK + j, n, stride=BS), :] for j in range(CHUNK)],
                axis=1,
            ).astype(jnp.bfloat16)
            right = chol_v[
                slot, :, pl.ds(pl.multiple_of(chunk * (CHUNK * BS), CHUNK * BS), CHUNK * BS)
            ]
            return acc + lax.dot_general(
                left, right, (((1,), (1,)), ((), ())), preferred_element_type=jnp.float32
            )

        term = lax.fori_loop(
            0, BS // CHUNK, bias_step, jnp.zeros((n, GS), jnp.float32), unroll=2
        )
        for block in range(nslab):
            cols = pl.ds(block * GS, GS)
            part[:, cols] = part[:, cols] + jnp.where(slab_ids(slab) == block, term, 0.0)

    parts_all[me] = part[...]
    each_peer(lambda dst: bias_copy(me, dst).start())
    each_peer(lambda src: field_copy(src, me).wait_recv())
    draws = jnp.concatenate([fields_all[walker] for walker in range(n)], axis=0)
    each_peer(lambda src: bias_copy(src, me).wait_recv())
    total = parts_all[0]
    for owner in range(1, n):
        total = total + parts_all[owner]
    total_ref[...] = total
    bias_ref[...] = total_ref[pl.ds(me, 1), :]
    shifted = draws - total

    for slot in range(TMAX):
        row, slab, valid = slot_facts(slot)
        scaled = valid * step_root
        picked = shifted[:, :GS]
        for block in range(1, nslab):
            picked = jnp.where(slab_ids(slab) == block, shifted[:, block * GS : (block + 1) * GS], picked)
        picked = picked.astype(jnp.bfloat16)

        def op_step(chunk, carry):
            right = chol_v[
                slot, :, pl.ds(pl.multiple_of(chunk * (CHUNK * BS), CHUNK * BS), CHUNK * BS)
            ]
            made = jnp.dot(picked, right, preferred_element_type=jnp.float32)
            for j in range(CHUNK):
                wide[pl.ds(chunk * CHUNK + j, n, stride=BS), :] = made[:, j * BS : (j + 1) * BS]
            return carry

        lax.fori_loop(0, BS // CHUNK, op_step, 0, unroll=2)

        def narrow_step(walker, carry):
            block = wide[pl.ds(pl.multiple_of(walker * BS, BS), BS), :]
            ops_out[slot, walker] = (block * scaled).astype(jnp.bfloat16)
            return carry

        lax.fori_loop(0, n, narrow_step, 0, unroll=4)
        each_peer(lambda dst: op_copy(slot, me, dst).start())
        ops_in[slot * n + me] = ops_out[slot, me]

    for slot in range(TMAX):
        each_peer(lambda src: op_copy(slot, src, me).wait_recv())
    for block in range(NBLOCK):
        cols = [c for c in (block - 1, block, block + 1) if 0 <= c < NBLOCK]
        total_rows = theta_ref[block].astype(jnp.float32)
        for slab in range(nslab):
            for col in cols:
                place = slot_of_ref[(slab * NBLOCK + block) * 3 + col - block + 1]
                total_rows = total_rows + jnp.dot(
                    ops_in[place],
                    theta_ref[col],
                    preferred_element_type=jnp.float32,
                )
        prop_ref[block] = total_rows.astype(jnp.bfloat16)

    each_peer(lambda dst: field_copy(me, dst).wait_send())
    each_peer(lambda dst: bias_copy(me, dst).wait_send())
    for slot in range(TMAX):
        each_peer(lambda dst: theta_copy(slot, me, dst).wait_send())
        each_peer(lambda dst: op_copy(slot, me, dst).wait_send())


def fused_bytes(n, nslab):
    block = BS * NOCC
    nchol = nslab * GS
    return (
        TMAX * GS * block * 2
        + 4 * TMAX * n * block * 2
        + n * block * 4
        + (n + 2) * n * nchol * 4
        + n * nchol * 32
        + 3 * NBLOCK * block * 2
    )


def per_device_fused(theta, trial, chol, fields, tile_info, tile_count, block_size):
    n = lax.axis_size("blk")
    nchol = fields.shape[1]
    nslab = nchol // GS
    slots = jnp.arange(n * TMAX, dtype=jnp.int32)
    live = slots % TMAX < tile_count[slots // TMAX]
    slab = jnp.arange(nslab, dtype=jnp.int32)[:, None, None, None]
    row = jnp.arange(NBLOCK, dtype=jnp.int32)[None, :, None, None]
    col = row + jnp.arange(-1, 2, dtype=jnp.int32)[None, None, :, None]
    match = (tile_info[0] == row) & (tile_info[1] == col) & (tile_info[2] == slab) & live
    places = (slots % TMAX) * n + slots // TMAX
    slot_of = jnp.sum(jnp.where(match, places, 0), axis=-1).reshape(-1)
    smem = pl.BlockSpec(memory_space=pltpu.SMEM)
    vmem = pl.BlockSpec(memory_space=pltpu.VMEM)
    dma = pltpu.SemaphoreType.DMA
    propagated, bias = pl.pallas_call(
        functools.partial(fused_kernel, n, nslab),
        out_shape=(
            jax.ShapeDtypeStruct((NBLOCK, BS, NOCC), jnp.bfloat16),
            jax.ShapeDtypeStruct((1, nchol), jnp.float32),
        ),
        in_specs=[smem] * 4 + [vmem] * 3 + [pl.BlockSpec(memory_space=pl.ANY)],
        out_specs=(vmem, vmem),
        scratch_shapes=[
            pltpu.VMEM((TMAX, GS, BS * BS), jnp.bfloat16),
            pltpu.VMEM((TMAX, n, BS, NOCC), jnp.bfloat16),
            pltpu.VMEM((TMAX, n, BS, NOCC), jnp.bfloat16),
            pltpu.VMEM((n * BS, BS), jnp.float32),
            pltpu.VMEM((n, nchol), jnp.float32),
            pltpu.VMEM((n, n, nchol), jnp.float32),
            pltpu.VMEM((n, nchol), jnp.float32),
            pltpu.VMEM((n, 1, nchol), jnp.float32),
            pltpu.VMEM((TMAX, n, BS, BS), jnp.bfloat16),
            pltpu.VMEM((TMAX * n, BS, BS), jnp.bfloat16),
            dma((TMAX,)),
            dma((TMAX, n)),
            dma((TMAX, n)),
            dma((n,)),
            dma((n,)),
            dma((n,)),
            dma((n,)),
            dma((TMAX, n)),
            dma((TMAX, n)),
        ],
        compiler_params=pltpu.CompilerParams(
            collective_id=0, has_side_effects=True, vmem_limit_bytes=VMEM_LIMIT
        ),
        name="afqmc_step",
    )(
        tile_info,
        tile_count,
        block_size,
        slot_of,
        theta.reshape(NBLOCK, BS, NOCC),
        trial.reshape(NBLOCK, BS, NOCC),
        fields,
        chol,
    )
    return (propagated.reshape(1, NBLOCK * BS, NOCC), bias)


def step(theta, trial, chol, fields, *tables):
    n = lax.axis_size("blk")
    small = fused_bytes(n, fields.shape[1] // GS) < VMEM_LIMIT * 3 // 4
    if theta.shape[0] == 1 and small:
        return per_device_fused(theta, trial, chol, fields, *tables)
    return per_device(theta, trial, chol, fields, *tables)


def per_device(theta, trial, chol, fields, tile_info, tile_count, block_size):
    owners = lax.axis_size("blk")
    owner_index = lax.axis_index("blk")
    walk_local = theta.shape[0]
    walkers = walk_local * owners
    slot_total = owners * TMAX
    nchol = fields.shape[1]
    zero_index = jnp.zeros((), jnp.int32)
    rows_valid = (jnp.arange(BS, dtype=jnp.int32)[None, :] < block_size[:, None]).astype(
        jnp.float32
    )
    slot_ids = jnp.arange(slot_total, dtype=jnp.int32)
    slot_live = (slot_ids % TMAX < tile_count[slot_ids // TMAX]).astype(jnp.float32)
    theta_blocks = theta.reshape(walk_local, NBLOCK, BS * NOCC)
    outgoing = jnp.take(theta_blocks, tile_info[1], axis=1).reshape(
        walk_local, owners, TMAX, BS * NOCC
    )
    received = lax.all_to_all(outgoing, "blk", split_axis=1, concat_axis=0, tiled=True).reshape(
        walkers, TMAX, BS, NOCC
    )
    own_info = lax.dynamic_slice(tile_info, (zero_index, owner_index * TMAX), (3, TMAX))
    own_live = lax.dynamic_slice(slot_live, (owner_index * TMAX,), (TMAX,))
    bias_local = jnp.zeros((walkers, nchol), jnp.float32)
    slot_masks = []
    for slot_index in range(TMAX):
        row_block = own_info[0, slot_index]
        col_block = own_info[1, slot_index]
        slab_index = own_info[2, slot_index]
        trial_rows = lax.dynamic_slice(trial, (row_block * BS, zero_index), (BS, NOCC))
        valid_mask = (
            rows_valid[row_block][:, None] * rows_valid[col_block][None, :] * own_live[slot_index]
        )
        green_block = (
            jnp.einsum(
                "pk,wqk->wpq",
                trial_rows,
                received[:, slot_index],
                preferred_element_type=jnp.float32,
            )
            * valid_mask
        ).astype(jnp.bfloat16)
        bias_term = jnp.einsum(
            "wf,gf->wg",
            green_block.reshape(walkers, BS * BS),
            chol[slot_index],
            preferred_element_type=jnp.float32,
        )
        current = lax.dynamic_slice(bias_local, (zero_index, slab_index * GS), (walkers, GS))
        bias_local = lax.dynamic_update_slice(
            bias_local, current + bias_term, (zero_index, slab_index * GS)
        )
        slot_masks.append(valid_mask)
    bias_all = lax.psum(bias_local, "blk")
    fields_all = lax.all_gather(fields, "blk", axis=0, tiled=True)
    shifted_all = (fields_all - bias_all).astype(jnp.bfloat16)
    own_bias = lax.dynamic_slice(
        bias_all, (owner_index * walk_local, zero_index), (walk_local, nchol)
    )
    operator_list = []
    for slot_index in range(TMAX):
        slab_index = own_info[2, slot_index]
        field_slab = lax.dynamic_slice(shifted_all, (zero_index, slab_index * GS), (walkers, GS))
        operator_block = (
            (
                jnp.dot(field_slab, chol[slot_index], preferred_element_type=jnp.float32)
                * step_root
            ).reshape(walkers, BS, BS)
            * slot_masks[slot_index]
        ).astype(jnp.bfloat16)
        operator_list.append(operator_block)
    stacked = jnp.stack(operator_list).reshape(TMAX, walkers, BS * BS)
    arrived = lax.all_to_all(stacked, "blk", split_axis=1, concat_axis=0, tiled=True).reshape(
        slot_total, walk_local, BS, BS
    )
    selected = jnp.take(theta.reshape(walk_local, NBLOCK, BS, NOCC), tile_info[1], axis=1)
    returned = jnp.einsum(
        "swpq,wsqk->swpk", arrived, selected, preferred_element_type=jnp.float32
    ).reshape(slot_total, walk_local, BS * NOCC)
    placement = (tile_info[0][:, None] == jnp.arange(NBLOCK, dtype=jnp.int32)[None, :]).astype(
        jnp.float32
    ) * slot_live[:, None]
    update = jnp.einsum("sb,swf->wbf", placement, returned, precision=lax.Precision.HIGHEST)
    propagated = (theta.astype(jnp.float32) + update.reshape(walk_local, NBLOCK * BS, NOCC)).astype(
        jnp.bfloat16
    )
    return (propagated, own_bias)


def solution(mesh):
    placed = (
        P(("grp", "blk"), None, None),
        P("grp", None),
        P(("grp", "blk"), None, None),
        P(("grp", "blk"), None),
        P("grp", None),
        P("grp"),
        P("grp"),
    )
    return jax.shard_map(
        step,
        mesh=mesh,
        in_specs=placed,
        out_specs=(P(("grp", "blk"), None, None), P(("grp", "blk"), None)),
        check_vma=False,
    )
```

```python
import functools

import jax
import jax.numpy as jnp
from jax import lax
from jax.experimental import pallas as pl
from jax.experimental.pallas import tpu as pltpu
from jax.sharding import PartitionSpec as P

BS = 128
NBLOCK = 8
NOCC = 128
GS = 128
TMAX = 2


step_root = 0.25

CHUNK = 8
PIECES = 2
ROWS = BS // PIECES
VMEM_LIMIT = 60000 * 1024
MESH = pl.DeviceIdType.MESH


def fused_kernel(
    n,
    nslab,
    info_ref,
    count_ref,
    size_ref,
    theta_ref,
    trial_ref,
    fields_ref,
    chol_ref,
    prop_ref,
    bias_ref,
    chol_v,
    staged,
    received,
    wide,
    part,
    parts_all,
    total_ref,
    fields_all,
    chol_sem,
    theta_send,
    theta_recv,
    field_send,
    field_recv,
    bias_send,
    bias_recv,
    op_send,
    op_recv,
    *pieces,
):
    ops_out, ops_in = pieces[:PIECES], pieces[PIECES:]
    me = lax.axis_index("blk")
    grp = lax.axis_index("grp")

    bits = n.bit_length() - 1

    def peer(step):
        if n != 1 << bits:
            return lax.rem(me + step, n)
        flips = n - step
        other = 0
        for k in range(bits):
            mine = lax.rem(me // (1 << k), 2)
            flip = lax.rem(flips // (1 << k), 2)
            other = other + lax.rem(mine + flip, 2) * (1 << k)
        return other

    def each_peer(body):
        def run(step, carry):
            body(peer(step))
            return carry

        lax.fori_loop(1, n, run, 0)

    def theta_copy(slot, src, dst):
        return pltpu.make_async_remote_copy(
            src_ref=staged.at[slot, dst],
            dst_ref=received.at[slot, src],
            send_sem=theta_send.at[slot, dst],
            recv_sem=theta_recv.at[slot, src],
            device_id=(grp, dst),
            device_id_type=MESH,
        )

    def field_copy(src, dst):
        return pltpu.make_async_remote_copy(
            src_ref=fields_ref,
            dst_ref=fields_all.at[src],
            send_sem=field_send.at[dst],
            recv_sem=field_recv.at[src],
            device_id=(grp, dst),
            device_id_type=MESH,
        )

    def bias_copy(src, dst):
        return pltpu.make_async_remote_copy(
            src_ref=part,
            dst_ref=parts_all.at[src],
            send_sem=bias_send.at[dst],
            recv_sem=bias_recv.at[src],
            device_id=(grp, dst),
            device_id_type=MESH,
        )

    def op_copy(piece, slot, src, dst):
        return pltpu.make_async_remote_copy(
            src_ref=ops_out[piece].at[slot, dst],
            dst_ref=ops_in[piece].at[slot * n + src],
            send_sem=op_send.at[piece, slot, dst],
            recv_sem=op_recv.at[piece, slot, src],
            device_id=(grp, dst),
            device_id_type=MESH,
        )

    barrier = pltpu.get_barrier_semaphore()
    each_peer(
        lambda dst: pl.semaphore_signal(
            barrier, inc=1, device_id=(grp, dst), device_id_type=MESH
        )
    )
    chol_loads = [
        pltpu.make_async_copy(chol_ref.at[slot], chol_v.at[slot], chol_sem.at[slot])
        for slot in range(TMAX)
    ]
    for load in chol_loads:
        load.start()

    def stage(owner, carry):
        for slot in range(TMAX):
            col = info_ref[1, owner * TMAX + slot]
            staged[slot, owner] = theta_ref[col]
        return carry

    lax.fori_loop(0, n, stage, 0)
    for slot in range(TMAX):
        received[slot, me] = staged[slot, me]
    fields_all[me] = fields_ref[...]
    part[...] = jnp.zeros_like(part)

    pl.semaphore_wait(barrier, n - 1)
    for slot in range(TMAX):
        each_peer(lambda dst: theta_copy(slot, me, dst).start())
        if slot == 0:
            each_peer(lambda dst: field_copy(me, dst).start())

    row_ids = lax.broadcasted_iota(jnp.int32, (BS, BS), 0)
    col_ids = lax.broadcasted_iota(jnp.int32, (BS, BS), 1)

    def slab_ids(slab):
        return jnp.broadcast_to(slab, (n, GS))

    def slot_facts(slot):
        own = me * TMAX + slot
        row = info_ref[0, own]
        col = info_ref[1, own]
        live = jnp.broadcast_to(count_ref[me], (BS, BS)) > slot
        valid = (row_ids < size_ref[row]) & (col_ids < size_ref[col]) & live
        return row, info_ref[2, own], valid.astype(jnp.float32)

    wanted = [
        (slab * NBLOCK + row) * NBLOCK + col
        for slab in range(nslab)
        for row in range(NBLOCK)
        for col in range(max(row - 1, 0), min(row + 2, NBLOCK))
    ]

    def find(owner, places):
        places = list(places)
        for slot in range(TMAX):
            own = owner * TMAX + slot
            code = (info_ref[2, own] * NBLOCK + info_ref[0, own]) * NBLOCK + info_ref[1, own]
            live = jnp.minimum(jnp.maximum(count_ref[owner] - slot, 0), 1)
            value = live * (slot * n + owner)
            for i, target in enumerate(wanted):
                off = code - target
                miss = jnp.minimum(jnp.maximum(off, -off), 1)
                places[i] = places[i] + value * (1 - miss)
        return tuple(places)

    places = lax.fori_loop(0, n, find, tuple(jnp.int32(0) for _ in wanted))
    place_of = dict(zip(wanted, places))

    for slot in range(TMAX):
        row, slab, valid = slot_facts(slot)
        trial_rows = trial_ref[row]

        def green_of(walker, carry):
            green = lax.dot_general(
                trial_rows,
                received[slot, walker],
                (((1,), (1,)), ((), ())),
                preferred_element_type=jnp.float32,
            )
            green = (green * valid).astype(jnp.bfloat16).astype(jnp.float32)
            wide[pl.ds(pl.multiple_of(walker * BS, BS), BS), :] = green

            return carry

        each_peer(lambda src: theta_copy(slot, src, me).wait_recv())
        lax.fori_loop(0, n, green_of, 0, unroll=4)
        chol_loads[slot].wait()

        def bias_step(chunk, acc):
            left = jnp.concatenate(
                [wide[pl.ds(chunk * CHUNK + j, n, stride=BS), :] for j in range(CHUNK)],
                axis=1,
            ).astype(jnp.bfloat16)
            right = chol_v[
                slot, :, pl.ds(pl.multiple_of(chunk * (CHUNK * BS), CHUNK * BS), CHUNK * BS)
            ]
            return acc + lax.dot_general(
                left, right, (((1,), (1,)), ((), ())), preferred_element_type=jnp.float32
            )

        term = lax.fori_loop(
            0, BS // CHUNK, bias_step, jnp.zeros((n, GS), jnp.float32), unroll=2
        )
        for block in range(nslab):
            cols = pl.ds(block * GS, GS)
            part[:, cols] = part[:, cols] + jnp.where(slab_ids(slab) == block, term, 0.0)

    parts_all[me] = part[...]
    each_peer(lambda dst: bias_copy(me, dst).start())
    each_peer(lambda src: field_copy(src, me).wait_recv())
    draws = jnp.concatenate([fields_all[walker] for walker in range(n)], axis=0)
    each_peer(lambda src: bias_copy(src, me).wait_recv())
    total = parts_all[0]
    for owner in range(1, n):
        total = total + parts_all[owner]
    total_ref[...] = total
    bias_ref[...] = total_ref[pl.ds(me, 1), :]
    shifted = draws - total

    facts = []
    for slot in range(TMAX):
        row, slab, valid = slot_facts(slot)
        picked = shifted[:, :GS]
        for block in range(1, nslab):
            cols = shifted[:, block * GS : (block + 1) * GS]
            picked = jnp.where(slab_ids(slab) == block, cols, picked)
        facts.append((picked.astype(jnp.bfloat16), valid * step_root))

    for piece in range(PIECES):
        for slot in range(TMAX):
            picked, scaled = facts[slot]
            scaled = scaled[piece * ROWS : (piece + 1) * ROWS]

            def op_step(chunk, carry):
                right = chol_v[
                    slot, :, pl.ds(pl.multiple_of(chunk * (CHUNK * BS), CHUNK * BS), CHUNK * BS)
                ]
                made = jnp.dot(picked, right, preferred_element_type=jnp.float32)
                for j in range(CHUNK):
                    wide[pl.ds(chunk * CHUNK + j, n, stride=BS), :] = made[
                        :, j * BS : (j + 1) * BS
                    ]
                return carry

            first = piece * (ROWS // CHUNK)
            lax.fori_loop(first, first + ROWS // CHUNK, op_step, 0, unroll=2)

            def narrow_step(walker, carry):
                start = pl.multiple_of(walker * BS + piece * ROWS, ROWS)
                block = wide[pl.ds(start, ROWS), :]
                ops_out[piece][slot, walker] = (block * scaled).astype(jnp.bfloat16)
                return carry

            lax.fori_loop(0, n, narrow_step, 0, unroll=4)
            each_peer(lambda dst: op_copy(piece, slot, me, dst).start())
            ops_in[piece][slot * n + me] = ops_out[piece][slot, me]

    for piece in range(PIECES):
        for slot in range(TMAX):
            each_peer(lambda src: op_copy(piece, slot, src, me).wait_recv())
        rows = pl.ds(piece * ROWS, ROWS)
        for block in range(NBLOCK):
            total_rows = theta_ref[block, rows, :].astype(jnp.float32)
            for slab in range(nslab):
                for col in range(max(block - 1, 0), min(block + 2, NBLOCK)):
                    place = place_of[(slab * NBLOCK + block) * NBLOCK + col]
                    total_rows = total_rows + jnp.dot(
                        ops_in[piece][place],
                        theta_ref[col],
                        preferred_element_type=jnp.float32,
                    )
            prop_ref[block, rows, :] = total_rows.astype(jnp.bfloat16)

    each_peer(lambda dst: field_copy(me, dst).wait_send())
    each_peer(lambda dst: bias_copy(me, dst).wait_send())
    for slot in range(TMAX):
        each_peer(lambda dst: theta_copy(slot, me, dst).wait_send())
        for piece in range(PIECES):
            each_peer(lambda dst: op_copy(piece, slot, me, dst).wait_send())


def fused_bytes(n, nslab):
    block = BS * NOCC
    nchol = nslab * GS
    return (
        TMAX * GS * block * 2
        + 4 * TMAX * n * block * 2
        + n * block * 4
        + (n + 2) * n * nchol * 4
        + n * nchol * 32
        + 3 * NBLOCK * block * 2
    )


def per_device_fused(theta, trial, chol, fields, tile_info, tile_count, block_size):
    n = lax.axis_size("blk")
    nchol = fields.shape[1]
    nslab = nchol // GS
    smem = pl.BlockSpec(memory_space=pltpu.SMEM)
    vmem = pl.BlockSpec(memory_space=pltpu.VMEM)
    dma = pltpu.SemaphoreType.DMA
    propagated, bias = pl.pallas_call(
        functools.partial(fused_kernel, n, nslab),
        out_shape=(
            jax.ShapeDtypeStruct((NBLOCK, BS, NOCC), jnp.bfloat16),
            jax.ShapeDtypeStruct((1, nchol), jnp.float32),
        ),
        in_specs=[smem] * 3 + [vmem] * 3 + [pl.BlockSpec(memory_space=pl.ANY)],
        out_specs=(vmem, vmem),
        scratch_shapes=[
            pltpu.VMEM((TMAX, GS, BS * BS), jnp.bfloat16),
            pltpu.VMEM((TMAX, n, BS, NOCC), jnp.bfloat16),
            pltpu.VMEM((TMAX, n, BS, NOCC), jnp.bfloat16),
            pltpu.VMEM((n * BS, BS), jnp.float32),
            pltpu.VMEM((n, nchol), jnp.float32),
            pltpu.VMEM((n, n, nchol), jnp.float32),
            pltpu.VMEM((n, nchol), jnp.float32),
            pltpu.VMEM((n, 1, nchol), jnp.float32),
            dma((TMAX,)),
            dma((TMAX, n)),
            dma((TMAX, n)),
            dma((n,)),
            dma((n,)),
            dma((n,)),
            dma((n,)),
            dma((PIECES, TMAX, n)),
            dma((PIECES, TMAX, n)),
            *[pltpu.VMEM((TMAX, n, ROWS, BS), jnp.bfloat16)] * PIECES,
            *[pltpu.VMEM((TMAX * n, ROWS, BS), jnp.bfloat16)] * PIECES,
        ],
        compiler_params=pltpu.CompilerParams(
            collective_id=0, has_side_effects=True, vmem_limit_bytes=VMEM_LIMIT
        ),
        name="afqmc_step",
    )(
        tile_info,
        tile_count,
        block_size,
        theta.reshape(NBLOCK, BS, NOCC),
        trial.reshape(NBLOCK, BS, NOCC),
        fields,
        chol,
    )
    return (propagated.reshape(1, NBLOCK * BS, NOCC), bias)


def step(theta, trial, chol, fields, *tables):
    n = lax.axis_size("blk")
    small = fused_bytes(n, fields.shape[1] // GS) < VMEM_LIMIT * 3 // 4
    if theta.shape[0] == 1 and small:
        return per_device_fused(theta, trial, chol, fields, *tables)
    return per_device(theta, trial, chol, fields, *tables)


def per_device(theta, trial, chol, fields, tile_info, tile_count, block_size):
    owners = lax.axis_size("blk")
    owner_index = lax.axis_index("blk")
    walk_local = theta.shape[0]
    walkers = walk_local * owners
    slot_total = owners * TMAX
    nchol = fields.shape[1]
    zero_index = jnp.zeros((), jnp.int32)
    rows_valid = (jnp.arange(BS, dtype=jnp.int32)[None, :] < block_size[:, None]).astype(
        jnp.float32
    )
    slot_ids = jnp.arange(slot_total, dtype=jnp.int32)
    slot_live = (slot_ids % TMAX < tile_count[slot_ids // TMAX]).astype(jnp.float32)
    theta_blocks = theta.reshape(walk_local, NBLOCK, BS * NOCC)
    outgoing = jnp.take(theta_blocks, tile_info[1], axis=1).reshape(
        walk_local, owners, TMAX, BS * NOCC
    )
    received = lax.all_to_all(outgoing, "blk", split_axis=1, concat_axis=0, tiled=True).reshape(
        walkers, TMAX, BS, NOCC
    )
    own_info = lax.dynamic_slice(tile_info, (zero_index, owner_index * TMAX), (3, TMAX))
    own_live = lax.dynamic_slice(slot_live, (owner_index * TMAX,), (TMAX,))
    bias_local = jnp.zeros((walkers, nchol), jnp.float32)
    slot_masks = []
    for slot_index in range(TMAX):
        row_block = own_info[0, slot_index]
        col_block = own_info[1, slot_index]
        slab_index = own_info[2, slot_index]
        trial_rows = lax.dynamic_slice(trial, (row_block * BS, zero_index), (BS, NOCC))
        valid_mask = (
            rows_valid[row_block][:, None] * rows_valid[col_block][None, :] * own_live[slot_index]
        )
        green_block = (
            jnp.einsum(
                "pk,wqk->wpq",
                trial_rows,
                received[:, slot_index],
                preferred_element_type=jnp.float32,
            )
            * valid_mask
        ).astype(jnp.bfloat16)
        bias_term = jnp.einsum(
            "wf,gf->wg",
            green_block.reshape(walkers, BS * BS),
            chol[slot_index],
            preferred_element_type=jnp.float32,
        )
        current = lax.dynamic_slice(bias_local, (zero_index, slab_index * GS), (walkers, GS))
        bias_local = lax.dynamic_update_slice(
            bias_local, current + bias_term, (zero_index, slab_index * GS)
        )
        slot_masks.append(valid_mask)
    bias_all = lax.psum(bias_local, "blk")
    fields_all = lax.all_gather(fields, "blk", axis=0, tiled=True)
    shifted_all = (fields_all - bias_all).astype(jnp.bfloat16)
    own_bias = lax.dynamic_slice(
        bias_all, (owner_index * walk_local, zero_index), (walk_local, nchol)
    )
    operator_list = []
    for slot_index in range(TMAX):
        slab_index = own_info[2, slot_index]
        field_slab = lax.dynamic_slice(shifted_all, (zero_index, slab_index * GS), (walkers, GS))
        operator_block = (
            (
                jnp.dot(field_slab, chol[slot_index], preferred_element_type=jnp.float32)
                * step_root
            ).reshape(walkers, BS, BS)
            * slot_masks[slot_index]
        ).astype(jnp.bfloat16)
        operator_list.append(operator_block)
    stacked = jnp.stack(operator_list).reshape(TMAX, walkers, BS * BS)
    arrived = lax.all_to_all(stacked, "blk", split_axis=1, concat_axis=0, tiled=True).reshape(
        slot_total, walk_local, BS, BS
    )
    selected = jnp.take(theta.reshape(walk_local, NBLOCK, BS, NOCC), tile_info[1], axis=1)
    returned = jnp.einsum(
        "swpq,wsqk->swpk", arrived, selected, preferred_element_type=jnp.float32
    ).reshape(slot_total, walk_local, BS * NOCC)
    placement = (tile_info[0][:, None] == jnp.arange(NBLOCK, dtype=jnp.int32)[None, :]).astype(
        jnp.float32
    ) * slot_live[:, None]
    update = jnp.einsum("sb,swf->wbf", placement, returned, precision=lax.Precision.HIGHEST)
    propagated = (theta.astype(jnp.float32) + update.reshape(walk_local, NBLOCK * BS, NOCC)).astype(
        jnp.bfloat16
    )
    return (propagated, own_bias)


def solution(mesh):
    placed = (
        P(("grp", "blk"), None, None),
        P("grp", None),
        P(("grp", "blk"), None, None),
        P(("grp", "blk"), None),
        P("grp", None),
        P("grp"),
        P("grp"),
    )
    return jax.shard_map(
        step,
        mesh=mesh,
        in_specs=placed,
        out_specs=(P(("grp", "blk"), None, None), P(("grp", "blk"), None)),
        check_vma=False,
    )
```

```python
import functools

import jax
import jax.numpy as jnp
from jax import lax
from jax.experimental import pallas as pl
from jax.experimental.pallas import tpu as pltpu
from jax.sharding import PartitionSpec as P

BS = 128
NBLOCK = 8
NOCC = 128
GS = 128
TMAX = 2


step_root = 0.25

CHUNK = 8
PIECES = 1
ROWS = BS // PIECES
VMEM_LIMIT = 60000 * 1024
MESH = pl.DeviceIdType.MESH


def fused_kernel(
    n,
    nslab,
    info_ref,
    count_ref,
    size_ref,
    theta_ref,
    trial_ref,
    fields_ref,
    chol_ref,
    prop_ref,
    bias_ref,
    chol_v,
    staged,
    received,
    wide,
    part,
    parts_all,
    total_ref,
    fields_all,
    chol_sem,
    theta_send,
    theta_recv,
    field_send,
    field_recv,
    bias_send,
    bias_recv,
    op_send,
    op_recv,
    *pieces,
):
    ops_out, ops_in = pieces[:PIECES], pieces[PIECES:]
    me = lax.axis_index("blk")
    grp = lax.axis_index("grp")

    bits = n.bit_length() - 1

    def peer(step):
        return lax.rem(me + step, n)
        flips = n - step
        other = 0
        for k in range(bits):
            mine = lax.rem(me // (1 << k), 2)
            flip = lax.rem(flips // (1 << k), 2)
            other = other + lax.rem(mine + flip, 2) * (1 << k)
        return other

    def each_peer(body):
        def run(step, carry):
            body(peer(step))
            return carry

        lax.fori_loop(1, n, run, 0)

    def theta_copy(slot, src, dst):
        return pltpu.make_async_remote_copy(
            src_ref=staged.at[slot, dst],
            dst_ref=received.at[slot, src],
            send_sem=theta_send.at[slot, dst],
            recv_sem=theta_recv.at[slot, src],
            device_id=(grp, dst),
            device_id_type=MESH,
        )

    def field_copy(src, dst):
        return pltpu.make_async_remote_copy(
            src_ref=fields_ref,
            dst_ref=fields_all.at[src],
            send_sem=field_send.at[dst],
            recv_sem=field_recv.at[src],
            device_id=(grp, dst),
            device_id_type=MESH,
        )

    def bias_copy(src, dst):
        return pltpu.make_async_remote_copy(
            src_ref=part,
            dst_ref=parts_all.at[src],
            send_sem=bias_send.at[dst],
            recv_sem=bias_recv.at[src],
            device_id=(grp, dst),
            device_id_type=MESH,
        )

    def op_copy(piece, slot, src, dst):
        return pltpu.make_async_remote_copy(
            src_ref=ops_out[piece].at[slot, dst],
            dst_ref=ops_in[piece].at[slot * n + src],
            send_sem=op_send.at[piece, slot, dst],
            recv_sem=op_recv.at[piece, slot, src],
            device_id=(grp, dst),
            device_id_type=MESH,
        )

    barrier = pltpu.get_barrier_semaphore()
    each_peer(
        lambda dst: pl.semaphore_signal(
            barrier, inc=1, device_id=(grp, dst), device_id_type=MESH
        )
    )
    chol_loads = [
        pltpu.make_async_copy(chol_ref.at[slot], chol_v.at[slot], chol_sem.at[slot])
        for slot in range(TMAX)
    ]
    for load in chol_loads:
        load.start()

    def stage(owner, carry):
        for slot in range(TMAX):
            col = info_ref[1, owner * TMAX + slot]
            staged[slot, owner] = theta_ref[col]
        return carry

    lax.fori_loop(0, n, stage, 0)
    for slot in range(TMAX):
        received[slot, me] = staged[slot, me]
    fields_all[me] = fields_ref[...]
    part[...] = jnp.zeros_like(part)

    pl.semaphore_wait(barrier, n - 1)
    for slot in range(TMAX):
        each_peer(lambda dst: theta_copy(slot, me, dst).start())
        if slot == 0:
            each_peer(lambda dst: field_copy(me, dst).start())

    row_ids = lax.broadcasted_iota(jnp.int32, (BS, BS), 0)
    col_ids = lax.broadcasted_iota(jnp.int32, (BS, BS), 1)

    def slab_ids(slab):
        return jnp.broadcast_to(slab, (n, GS))

    def slot_facts(slot):
        own = me * TMAX + slot
        row = info_ref[0, own]
        col = info_ref[1, own]
        live = jnp.broadcast_to(count_ref[me], (BS, BS)) > slot
        valid = (row_ids < size_ref[row]) & (col_ids < size_ref[col]) & live
        return row, info_ref[2, own], valid.astype(jnp.float32)

    wanted = [
        (slab * NBLOCK + row) * NBLOCK + col
        for slab in range(nslab)
        for row in range(NBLOCK)
        for col in range(max(row - 1, 0), min(row + 2, NBLOCK))
    ]

    def find(owner, places):
        places = list(places)
        for slot in range(TMAX):
            own = owner * TMAX + slot
            code = (info_ref[2, own] * NBLOCK + info_ref[0, own]) * NBLOCK + info_ref[1, own]
            live = jnp.minimum(jnp.maximum(count_ref[owner] - slot, 0), 1)
            value = live * (slot * n + owner)
            for i, target in enumerate(wanted):
                off = code - target
                miss = jnp.minimum(jnp.maximum(off, -off), 1)
                places[i] = places[i] + value * (1 - miss)
        return tuple(places)

    places = lax.fori_loop(0, n, find, tuple(jnp.int32(0) for _ in wanted))
    place_of = dict(zip(wanted, places))

    for slot in range(TMAX):
        row, slab, valid = slot_facts(slot)
        trial_rows = trial_ref[row]

        def green_of(walker, carry):
            green = lax.dot_general(
                trial_rows,
                received[slot, walker],
                (((1,), (1,)), ((), ())),
                preferred_element_type=jnp.float32,
            )
            green = (green * valid).astype(jnp.bfloat16).astype(jnp.float32)
            wide[pl.ds(pl.multiple_of(walker * BS, BS), BS), :] = green

            return carry

        each_peer(lambda src: theta_copy(slot, src, me).wait_recv())
        lax.fori_loop(0, n, green_of, 0, unroll=8)
        chol_loads[slot].wait()

        def bias_step(chunk, acc):
            left = jnp.concatenate(
                [wide[pl.ds(chunk * CHUNK + j, n, stride=BS), :] for j in range(CHUNK)],
                axis=1,
            ).astype(jnp.bfloat16)
            right = chol_v[
                slot, :, pl.ds(pl.multiple_of(chunk * (CHUNK * BS), CHUNK * BS), CHUNK * BS)
            ]
            return acc + lax.dot_general(
                left, right, (((1,), (1,)), ((), ())), preferred_element_type=jnp.float32
            )

        term = lax.fori_loop(
            0, BS // CHUNK, bias_step, jnp.zeros((n, GS), jnp.float32), unroll=8
        )
        for block in range(nslab):
            cols = pl.ds(block * GS, GS)
            part[:, cols] = part[:, cols] + jnp.where(slab_ids(slab) == block, term, 0.0)

    parts_all[me] = part[...]
    each_peer(lambda dst: bias_copy(me, dst).start())
    each_peer(lambda src: field_copy(src, me).wait_recv())
    draws = jnp.concatenate([fields_all[walker] for walker in range(n)], axis=0)
    each_peer(lambda src: bias_copy(src, me).wait_recv())
    total = parts_all[0]
    for owner in range(1, n):
        total = total + parts_all[owner]
    total_ref[...] = total
    bias_ref[...] = total_ref[pl.ds(me, 1), :]
    shifted = draws - total

    facts = []
    for slot in range(TMAX):
        row, slab, valid = slot_facts(slot)
        picked = shifted[:, :GS]
        for block in range(1, nslab):
            cols = shifted[:, block * GS : (block + 1) * GS]
            picked = jnp.where(slab_ids(slab) == block, cols, picked)
        facts.append((picked.astype(jnp.bfloat16), valid * step_root))

    for piece in range(PIECES):
        for slot in range(TMAX):
            picked, scaled = facts[slot]
            scaled = scaled[piece * ROWS : (piece + 1) * ROWS]

            def op_step(chunk, carry):
                right = chol_v[
                    slot, :, pl.ds(pl.multiple_of(chunk * (CHUNK * BS), CHUNK * BS), CHUNK * BS)
                ]
                made = jnp.dot(picked, right, preferred_element_type=jnp.float32)
                for j in range(CHUNK):
                    wide[pl.ds(chunk * CHUNK + j, n, stride=BS), :] = made[
                        :, j * BS : (j + 1) * BS
                    ]
                return carry

            first = piece * (ROWS // CHUNK)
            lax.fori_loop(first, first + ROWS // CHUNK, op_step, 0, unroll=8)

            def narrow_step(walker, carry):
                start = pl.multiple_of(walker * BS + piece * ROWS, ROWS)
                block = wide[pl.ds(start, ROWS), :]
                ops_out[piece][slot, walker] = (block * scaled).astype(jnp.bfloat16)
                return carry

            lax.fori_loop(0, n, narrow_step, 0, unroll=4)
            each_peer(lambda dst: op_copy(piece, slot, me, dst).start())
            ops_in[piece][slot * n + me] = ops_out[piece][slot, me]

    for piece in range(PIECES):
        for slot in range(TMAX):
            each_peer(lambda src: op_copy(piece, slot, src, me).wait_recv())
        rows = pl.ds(piece * ROWS, ROWS)
        for block in range(NBLOCK):
            total_rows = theta_ref[block, rows, :].astype(jnp.float32)
            for slab in range(nslab):
                for col in range(max(block - 1, 0), min(block + 2, NBLOCK)):
                    place = place_of[(slab * NBLOCK + block) * NBLOCK + col]
                    total_rows = total_rows + jnp.dot(
                        ops_in[piece][place],
                        theta_ref[col],
                        preferred_element_type=jnp.float32,
                    )
            prop_ref[block, rows, :] = total_rows.astype(jnp.bfloat16)

    each_peer(lambda dst: field_copy(me, dst).wait_send())
    each_peer(lambda dst: bias_copy(me, dst).wait_send())
    for slot in range(TMAX):
        each_peer(lambda dst: theta_copy(slot, me, dst).wait_send())
        for piece in range(PIECES):
            each_peer(lambda dst: op_copy(piece, slot, me, dst).wait_send())


def fused_bytes(n, nslab):
    block = BS * NOCC
    nchol = nslab * GS
    return (
        TMAX * GS * block * 2
        + 4 * TMAX * n * block * 2
        + n * block * 4
        + (n + 2) * n * nchol * 4
        + n * nchol * 32
        + 3 * NBLOCK * block * 2
    )


def per_device_fused(theta, trial, chol, fields, tile_info, tile_count, block_size):
    n = lax.axis_size("blk")
    nchol = fields.shape[1]
    nslab = nchol // GS
    smem = pl.BlockSpec(memory_space=pltpu.SMEM)
    vmem = pl.BlockSpec(memory_space=pltpu.VMEM)
    dma = pltpu.SemaphoreType.DMA
    propagated, bias = pl.pallas_call(
        functools.partial(fused_kernel, n, nslab),
        out_shape=(
            jax.ShapeDtypeStruct((NBLOCK, BS, NOCC), jnp.bfloat16),
            jax.ShapeDtypeStruct((1, nchol), jnp.float32),
        ),
        in_specs=[smem] * 3 + [vmem] * 3 + [pl.BlockSpec(memory_space=pl.ANY)],
        out_specs=(vmem, vmem),
        scratch_shapes=[
            pltpu.VMEM((TMAX, GS, BS * BS), jnp.bfloat16),
            pltpu.VMEM((TMAX, n, BS, NOCC), jnp.bfloat16),
            pltpu.VMEM((TMAX, n, BS, NOCC), jnp.bfloat16),
            pltpu.VMEM((n * BS, BS), jnp.float32),
            pltpu.VMEM((n, nchol), jnp.float32),
            pltpu.VMEM((n, n, nchol), jnp.float32),
            pltpu.VMEM((n, nchol), jnp.float32),
            pltpu.VMEM((n, 1, nchol), jnp.float32),
            dma((TMAX,)),
            dma((TMAX, n)),
            dma((TMAX, n)),
            dma((n,)),
            dma((n,)),
            dma((n,)),
            dma((n,)),
            dma((PIECES, TMAX, n)),
            dma((PIECES, TMAX, n)),
            *[pltpu.VMEM((TMAX, n, ROWS, BS), jnp.bfloat16)] * PIECES,
            *[pltpu.VMEM((TMAX * n, ROWS, BS), jnp.bfloat16)] * PIECES,
        ],
        compiler_params=pltpu.CompilerParams(
            collective_id=0, has_side_effects=True, vmem_limit_bytes=VMEM_LIMIT
        ),
        name="afqmc_step",
    )(
        tile_info,
        tile_count,
        block_size,
        theta.reshape(NBLOCK, BS, NOCC),
        trial.reshape(NBLOCK, BS, NOCC),
        fields,
        chol,
    )
    return (propagated.reshape(1, NBLOCK * BS, NOCC), bias)


def step(theta, trial, chol, fields, *tables):
    n = lax.axis_size("blk")
    small = fused_bytes(n, fields.shape[1] // GS) < VMEM_LIMIT * 3 // 4
    if theta.shape[0] == 1 and small:
        return per_device_fused(theta, trial, chol, fields, *tables)
    return per_device(theta, trial, chol, fields, *tables)


def per_device(theta, trial, chol, fields, tile_info, tile_count, block_size):
    owners = lax.axis_size("blk")
    owner_index = lax.axis_index("blk")
    walk_local = theta.shape[0]
    walkers = walk_local * owners
    slot_total = owners * TMAX
    nchol = fields.shape[1]
    zero_index = jnp.zeros((), jnp.int32)
    rows_valid = (jnp.arange(BS, dtype=jnp.int32)[None, :] < block_size[:, None]).astype(
        jnp.float32
    )
    slot_ids = jnp.arange(slot_total, dtype=jnp.int32)
    slot_live = (slot_ids % TMAX < tile_count[slot_ids // TMAX]).astype(jnp.float32)
    theta_blocks = theta.reshape(walk_local, NBLOCK, BS * NOCC)
    outgoing = jnp.take(theta_blocks, tile_info[1], axis=1).reshape(
        walk_local, owners, TMAX, BS * NOCC
    )
    received = lax.all_to_all(outgoing, "blk", split_axis=1, concat_axis=0, tiled=True).reshape(
        walkers, TMAX, BS, NOCC
    )
    own_info = lax.dynamic_slice(tile_info, (zero_index, owner_index * TMAX), (3, TMAX))
    own_live = lax.dynamic_slice(slot_live, (owner_index * TMAX,), (TMAX,))
    bias_local = jnp.zeros((walkers, nchol), jnp.float32)
    slot_masks = []
    for slot_index in range(TMAX):
        row_block = own_info[0, slot_index]
        col_block = own_info[1, slot_index]
        slab_index = own_info[2, slot_index]
        trial_rows = lax.dynamic_slice(trial, (row_block * BS, zero_index), (BS, NOCC))
        valid_mask = (
            rows_valid[row_block][:, None] * rows_valid[col_block][None, :] * own_live[slot_index]
        )
        green_block = (
            jnp.einsum(
                "pk,wqk->wpq",
                trial_rows,
                received[:, slot_index],
                preferred_element_type=jnp.float32,
            )
            * valid_mask
        ).astype(jnp.bfloat16)
        bias_term = jnp.einsum(
            "wf,gf->wg",
            green_block.reshape(walkers, BS * BS),
            chol[slot_index],
            preferred_element_type=jnp.float32,
        )
        current = lax.dynamic_slice(bias_local, (zero_index, slab_index * GS), (walkers, GS))
        bias_local = lax.dynamic_update_slice(
            bias_local, current + bias_term, (zero_index, slab_index * GS)
        )
        slot_masks.append(valid_mask)
    bias_all = lax.psum(bias_local, "blk")
    fields_all = lax.all_gather(fields, "blk", axis=0, tiled=True)
    shifted_all = (fields_all - bias_all).astype(jnp.bfloat16)
    own_bias = lax.dynamic_slice(
        bias_all, (owner_index * walk_local, zero_index), (walk_local, nchol)
    )
    operator_list = []
    for slot_index in range(TMAX):
        slab_index = own_info[2, slot_index]
        field_slab = lax.dynamic_slice(shifted_all, (zero_index, slab_index * GS), (walkers, GS))
        operator_block = (
            (
                jnp.dot(field_slab, chol[slot_index], preferred_element_type=jnp.float32)
                * step_root
            ).reshape(walkers, BS, BS)
            * slot_masks[slot_index]
        ).astype(jnp.bfloat16)
        operator_list.append(operator_block)
    stacked = jnp.stack(operator_list).reshape(TMAX, walkers, BS * BS)
    arrived = lax.all_to_all(stacked, "blk", split_axis=1, concat_axis=0, tiled=True).reshape(
        slot_total, walk_local, BS, BS
    )
    selected = jnp.take(theta.reshape(walk_local, NBLOCK, BS, NOCC), tile_info[1], axis=1)
    returned = jnp.einsum(
        "swpq,wsqk->swpk", arrived, selected, preferred_element_type=jnp.float32
    ).reshape(slot_total, walk_local, BS * NOCC)
    placement = (tile_info[0][:, None] == jnp.arange(NBLOCK, dtype=jnp.int32)[None, :]).astype(
        jnp.float32
    ) * slot_live[:, None]
    update = jnp.einsum("sb,swf->wbf", placement, returned, precision=lax.Precision.HIGHEST)
    propagated = (theta.astype(jnp.float32) + update.reshape(walk_local, NBLOCK * BS, NOCC)).astype(
        jnp.bfloat16
    )
    return (propagated, own_bias)


def solution(mesh):
    placed = (
        P(("grp", "blk"), None, None),
        P("grp", None),
        P(("grp", "blk"), None, None),
        P(("grp", "blk"), None),
        P("grp", None),
        P("grp"),
        P("grp"),
    )
    return jax.shard_map(
        step,
        mesh=mesh,
        in_specs=placed,
        out_specs=(P(("grp", "blk"), None, None), P(("grp", "blk"), None)),
        check_vma=False,
    )
```
